32 devices in a mesh: tile: 8 (over z, core), layer: 4 (over y, x).
Axes of the slice: x: 2, y: 2, z: 4, core: 2. Of those that a mesh axis runs over, the one named last changes fastest.
Arguments:
- basis: float32 [8, 768, 32], P('tile'), may hold values from -0.21875 to 0.21875
- ranks: int32 [8], P('tile'), may hold values from 8 to 32
- cores: float32 [8, 8, 32, 32], P('tile', 'layer'), may hold values from -1.11 to 1.11
- diag: float32 [8, 768, 768], P('tile', 'layer'), may hold values from 0 to 9, as said below
Outputs:
- factors: float32 [1, 768, 768], P(None, 'layer')
- panel_basis: float32 [1, 768, 32], replicated
- schur_diag: float32 [8, 768, 768], P('tile', 'layer')
- schur_cores: float32 [8, 8, 32, 32], P('tile', 'layer')
The draws below stay inside these ranges and needn't reach their ends.
Inputs may be any that keep to these rules, and one draw needn't show every extreme that they name: `diag`: each tile is a Gaussian kernel of points in the unit cube plus a multiple of the identity, so symmetric positive definite.
All inputs are finite; a program needn't handle non-finite values.
Results may differ from the reference program's by a relative error of at most 0.0001.
Values sent between devices are 32-bit elements; how exact they have to be, the bound alone decides.
A program may use at most 64 MiB of HBM per device.

```python
import jax
import jax.numpy as jnp
from jax import lax

TS = 768
RMAX = 32
PANELS = 1
NT = 8


def draw_diag(key, part):
    points = jax.random.uniform(key, (NT, TS, 3), jnp.float32)
    spread = 0.25
    nugget = 8.0
    norms = jnp.sum(points * points, axis=-1)
    cross = jnp.einsum('tad,tbd->tab', points, points, precision=jax.lax.Precision.HIGHEST)
    dist = jnp.maximum(norms[:, :, None] + norms[:, None, :] - 2.0 * cross, 0.0)
    kernel = jnp.exp(-dist / (2.0 * spread * spread))
    return kernel + nugget * jnp.eye(TS, dtype=jnp.float32)[None]


def draw_cores(key, part):
    spread = 0.37
    values = jax.random.normal(key, (NT, NT, RMAX, RMAX), jnp.float32)
    values = jnp.clip(values, -3.0, 3.0) * spread
    return values


def set_ends(entries, own_key, least, high):
    place = [jax.random.randint(jax.random.fold_in(own_key, axis), (), 0, length) for axis, length in enumerate(entries.shape)]
    longest = entries.shape.index(max(entries.shape))
    next_to = place[:longest] + [(place[longest] + 1) % entries.shape[longest]] + place[longest + 1:]
    return entries.at[tuple(place)].set(least).at[tuple(next_to)].set(high)


def steps_of(rng, extent, split, low, high):
    level, own = 1.0, jax.random.fold_in(rng, 6)
    for dim, shards_of in split:
        steps = jnp.exp(jax.random.uniform(jax.random.fold_in(own, dim), (shards_of,), jnp.float32, low / len(split), high / len(split)))
        level = level * jnp.repeat(steps, extent[dim] // shards_of).reshape([-1 if axis == dim else 1 for axis in range(len(extent))])
    return level


def gaussian(key, shape, scale, limit, shards=(), kind=jnp.bfloat16):
    level = steps_of(key, shape, shards, -0.22, 0.18) if shards else 1.0
    values = jax.random.normal(key, shape, jnp.float32) * scale * level
    return jnp.minimum(jnp.maximum(values, -limit), limit).astype(kind)


def setup_inputs(seed: int = 0) -> dict:
    arg_keys = jax.random.split(jax.random.key(seed), 5)
    return {
        "basis": gaussian(arg_keys[0], (NT, TS, RMAX), TS ** -0.5, 0.21875, ((0, 8),), jnp.float32),
        "ranks": set_ends(jax.random.randint(arg_keys[1], (NT,), RMAX // 4, RMAX + 1), jax.random.fold_in(arg_keys[1], 1), RMAX // 4, RMAX).astype(jnp.int32),
        "cores": draw_cores(jax.random.fold_in(arg_keys[4], 71), 0),
        "diag": draw_diag(jax.random.fold_in(arg_keys[4], 71), 0),
    }


HI = lax.Precision.HIGHEST

def factor(tile, panel_u):
    lower = jnp.linalg.cholesky(tile)
    solved = lax.linalg.triangular_solve(lower, panel_u, left_side=True, lower=True)
    gram = jnp.dot(solved.T, solved, precision=HI)
    return (lower, solved, gram)

def reference(basis, ranks, cores, diag):
    keep = (jnp.arange(RMAX, dtype=jnp.int32)[None, :] < ranks[:, None]).astype(jnp.float32)
    masked = basis * keep[:, None, :]
    ids = jnp.arange(NT, dtype=jnp.int32)
    factors = []
    bases = []
    for panel in range(PANELS):
        lower, solved, gram = factor(diag[panel], masked[panel])
        factors.append(lower)
        bases.append(solved)
        column = cores[:, panel]
        coef = jnp.einsum('trs,su->tru', column, gram, precision=HI)
        inner = jnp.einsum('tru,tvu->trv', coef, column, precision=HI)
        partial_rows = jnp.einsum('tar,trv->tav', masked, inner, precision=HI)
        change = jnp.einsum('tav,tbv->tab', partial_rows, masked, precision=HI)
        diag = diag - jnp.where((ids > panel)[:, None, None], change, 0.0)
        pair = jnp.einsum('tru,cvu->tcrv', coef, column, precision=HI)
        live = (ids[:, None] > ids[None, :]) & (ids[None, :] > panel)
        cores = cores - jnp.where(live[:, :, None, None], pair, 0.0)
    return (jnp.stack(factors), jnp.stack(bases), diag, cores)
```

```python
import jax
import jax.numpy as jnp
from jax import lax
from jax.experimental import pallas as pl
from jax.experimental.pallas import tpu as pltpu
from jax.sharding import PartitionSpec as P

HI = lax.Precision.HIGHEST
B = 128
S = 8


def nt(a, b):
    return lax.dot_general(
        a, b, (((1,), (1,)), ((), ())), precision=HI, preferred_element_type=jnp.float32
    )


def nn(a, b):
    return jnp.dot(a, b, precision=HI, preferred_element_type=jnp.float32)


def total(terms):
    while len(terms) > 1:
        terms = [
            terms[i] + terms[i + 1] if i + 1 < len(terms) else terms[i]
            for i in range(0, len(terms), 2)
        ]
    return terms[0]


def spread_lane(block, lane):
    return jnp.broadcast_to(block[:, lane : lane + 1], (S, B))


def spread_row(block, row):
    return jnp.broadcast_to(block[row : row + 1, :], (S, B))


def base_factor(tile_ref, upper_ref, inv_ref):
    groups = B // S
    sub = lax.broadcasted_iota(jnp.int32, (S, B), 0)
    lane = lax.broadcasted_iota(jnp.int32, (S, B), 1)
    left = [tile_ref[S * g : S * g + S, :] for g in range(groups)]
    right = [jnp.where(lane == sub + S * g, 1.0, 0.0) for g in range(groups)]
    for b in range(groups):
        a, q = left[b], right[b]
        cols = [spread_lane(a, S * b + j) for j in range(S)]
        e = [[spread_row(cols[j], i) if j <= i else None for j in range(S)] for i in range(S)]
        inv, low = [], [[None] * S for _ in range(S)]
        for j in range(S):
            inv.append(1.0 / e[j][j])
            for i in range(j + 1, S):
                low[i][j] = e[i][j] * inv[j]
            for k in range(j + 1, S):
                for i in range(k, S):
                    e[i][k] = e[i][k] - low[i][j] * e[k][j]
        ra = [spread_row(a, i) for i in range(S)]
        rq = [spread_row(q, i) for i in range(S)]
        for j in range(S):
            for i in range(j + 1, S):
                ra[i] = ra[i] - low[i][j] * ra[j]
                rq[i] = rq[i] - low[i][j] * rq[j]
        xa, xq = None, None
        for j in range(S):
            root = lax.rsqrt(e[j][j])
            ya, yq = ra[j] * root, rq[j] * root
            xa = ya if xa is None else jnp.where(sub == j, ya, xa)
            xq = yq if xq is None else jnp.where(sub == j, yq, xq)
        upper_ref[S * b : S * b + S, :] = jnp.where(lane >= sub + S * b, xa, 0.0)
        inv_ref[S * b : S * b + S, :] = xq
        if b + 1 == groups:
            break
        wa = [ra[j] * inv[j] for j in range(S)]
        wq = [rq[j] * inv[j] for j in range(S)]
        for i in range(S - 1, 0, -1):
            for j in range(i):
                wa[j] = wa[j] - low[i][j] * wa[i]
                wq[j] = wq[j] - low[i][j] * wq[i]
        for g in range(b + 1, groups):
            m = [spread_lane(left[g], S * b + j) for j in range(S)]
            left[g] = left[g] - total([m[j] * wa[j] for j in range(S)])
            right[g] = right[g] - total([m[j] * wq[j] for j in range(S)])


def chol_kernel(tile_ref, u_ref, lower_ref, z_ref, work, block, upper, inverse):
    order = tile_ref.shape[0]
    panels = order // B
    work[...] = tile_ref[...]
    z_ref[...] = u_ref[...]
    lower_ref[...] = jnp.zeros_like(lower_ref)

    def panel(k, carry):
        at = pl.ds(pl.multiple_of(k * B, B), B)
        block[...] = work[at, at]
        base_factor(block, upper, inverse)
        lower_ref[at, at] = upper[...].T
        z = nn(inverse[...], z_ref[at, :])
        z_ref[at, :] = z
        for c in range(panels - 1):
            @pl.when(k == c)
            def _():
                here = slice(c * B, c * B + B)
                rest = slice(c * B + B, order)
                below = nt(work[rest, here], inverse[...])
                lower_ref[rest, here] = below
                z_ref[rest, :] = z_ref[rest, :] - nn(below, z)
                for j in range(c + 1, panels):
                    cols = slice(j * B, j * B + B)
                    rows = slice(j * B, order)
                    own = below[(j - c - 1) * B :, :]
                    work[rows, cols] = work[rows, cols] - nt(own, own[:B, :])
        return carry

    lax.fori_loop(0, panels, panel, 0)


def factor(tile, panel_u):
    order, rank = panel_u.shape
    vm = pl.BlockSpec(memory_space=pltpu.VMEM)
    return pl.pallas_call(
        chol_kernel,
        out_shape=(
            jax.ShapeDtypeStruct((order, order), jnp.float32),
            jax.ShapeDtypeStruct((order, rank), jnp.float32),
        ),
        in_specs=[vm, vm],
        out_specs=(vm, vm),
        scratch_shapes=[
            pltpu.VMEM((order, order), jnp.float32),
            pltpu.VMEM((B, B), jnp.float32),
            pltpu.VMEM((B, B), jnp.float32),
            pltpu.VMEM((B, B), jnp.float32),
        ],
    )(tile, panel_u)


def broadcast(value, axis, source):
    kept = jnp.where(lax.axis_index(axis) == source, value, 0).astype(value.dtype)
    return lax.psum(kept, axis)


def body(basis, ranks, cores, diag):
    tile_dev = basis.shape[0]
    rmax = basis.shape[2]
    span = cores.shape[1]
    tile_rows = diag.shape[1]
    my_tile = lax.axis_index("tile")
    my_layer = lax.axis_index("layer")
    row_ids = my_tile * tile_dev + jnp.arange(tile_dev, dtype=jnp.int32)
    col_ids = my_layer * span + jnp.arange(span, dtype=jnp.int32)
    keep = (jnp.arange(rmax, dtype=jnp.int32)[None, :] < ranks[:, None]).astype(jnp.float32)
    masked = basis * keep[:, None, :]
    basis_rows = lax.dynamic_slice_in_dim(masked, my_layer * tile_rows, tile_rows, 1)
    rows_piece = broadcast(diag[0], "tile", 0)
    panel_u = broadcast(masked[0], "tile", 0)
    whole = lax.all_gather(rows_piece, "layer", axis=0, tiled=True)
    lower, solved = factor(whole, panel_u)
    gram = jnp.dot(solved.T, solved, precision=HI)
    lower_rows = lax.dynamic_slice_in_dim(lower, my_layer * tile_rows, tile_rows, 0)
    column = broadcast(cores[:, 0], "layer", 0)
    full_column = lax.all_gather(column, "tile", axis=0, tiled=True)
    others = lax.dynamic_slice_in_dim(full_column, my_layer * span, span, 0)
    coef = jnp.einsum("trs,su->tru", column, gram, precision=HI)
    inner = jnp.einsum("tru,tvu->trv", coef, column, precision=HI)
    partial_rows = jnp.einsum("tar,trv->tav", basis_rows, inner, precision=HI)
    change = jnp.einsum("tav,tbv->tab", partial_rows, masked, precision=HI)
    diag = diag - jnp.where((row_ids > 0)[:, None, None], change, 0.0)
    pair = jnp.einsum("tru,cvu->tcrv", coef, others, precision=HI)
    live = (row_ids[:, None] > col_ids[None, :]) & (col_ids[None, :] > 0)
    cores = cores - jnp.where(live[:, :, None, None], pair, 0.0)
    return (lower_rows[None], solved[None], diag, cores)


def solution(mesh):
    placed = (
        P("tile", None, None),
        P("tile"),
        P("tile", "layer", None, None),
        P("tile", "layer", None),
    )
    return jax.shard_map(
        body,
        mesh=mesh,
        in_specs=placed,
        out_specs=(
            P(None, "layer", None),
            P(),
            P("tile", "layer", None),
            P("tile", "layer", None, None),
        ),
        check_vma=False,
    )
```

```python
import functools

import jax
import jax.numpy as jnp
from jax import lax
from jax.experimental import pallas as pl
from jax.experimental.pallas import tpu as pltpu
from jax.sharding import PartitionSpec as P

HI = lax.Precision.HIGHEST
B = 128
S = 8


def nt(a, b):
    return lax.dot_general(
        a, b, (((1,), (1,)), ((), ())), precision=HI, preferred_element_type=jnp.float32
    )


def nn(a, b):
    return jnp.dot(a, b, precision=HI, preferred_element_type=jnp.float32)


def total(terms):
    while len(terms) > 1:
        terms = [
            terms[i] + terms[i + 1] if i + 1 < len(terms) else terms[i]
            for i in range(0, len(terms), 2)
        ]
    return terms[0]


def spread_lane(block, lane):
    return jnp.broadcast_to(block[:, lane : lane + 1], (S, B))


def spread_row(block, row):
    return jnp.broadcast_to(block[row : row + 1, :], (S, B))


def base_factor(tile_ref, upper_ref, inv_ref, midway):
    groups = B // S
    sub = lax.broadcasted_iota(jnp.int32, (S, B), 0)
    lane = lax.broadcasted_iota(jnp.int32, (S, B), 1)
    left = [tile_ref[S * g : S * g + S, :] for g in range(groups)]
    right = [jnp.where(lane == sub + S * g, 1.0, 0.0) for g in range(groups)]
    for b in range(groups):
        if b == groups // 2:
            midway()
        a, q = left[b], right[b]
        cols = [spread_lane(a, S * b + j) for j in range(S)]
        e = [[spread_row(cols[j], i) if j <= i else None for j in range(S)] for i in range(S)]
        inv, low = [], [[None] * S for _ in range(S)]
        for j in range(S):
            inv.append(1.0 / e[j][j])
            for i in range(j + 1, S):
                low[i][j] = e[i][j] * inv[j]
            for k in range(j + 1, S):
                for i in range(k, S):
                    e[i][k] = e[i][k] - low[i][j] * e[k][j]
        ra = [spread_row(a, i) for i in range(S)]
        rq = [spread_row(q, i) for i in range(S)]
        for j in range(S):
            for i in range(j + 1, S):
                ra[i] = ra[i] - low[i][j] * ra[j]
                rq[i] = rq[i] - low[i][j] * rq[j]
        xa, xq = None, None
        for j in range(S):
            root = lax.rsqrt(e[j][j])
            ya, yq = ra[j] * root, rq[j] * root
            xa = ya if xa is None else jnp.where(sub == j, ya, xa)
            xq = yq if xq is None else jnp.where(sub == j, yq, xq)
        upper_ref[S * b : S * b + S, :] = jnp.where(lane >= sub + S * b, xa, 0.0)
        inv_ref[S * b : S * b + S, :] = xq
        if b + 1 == groups:
            break
        wa = [ra[j] * inv[j] for j in range(S)]
        wq = [rq[j] * inv[j] for j in range(S)]
        for i in range(S - 1, 0, -1):
            for j in range(i):
                wa[j] = wa[j] - low[i][j] * wa[i]
                wq[j] = wq[j] - low[i][j] * wq[i]
        for g in range(b + 1, groups):
            m = [spread_lane(left[g], S * b + j) for j in range(S)]
            left[g] = left[g] - total([m[j] * wa[j] for j in range(S)])
            right[g] = right[g] - total([m[j] * wq[j] for j in range(S)])


def panel_kernel(
    tiles, layers, diag_ref, masked_ref, masked_t_ref, cores_ref,
    factor_ref, z_ref, diag_out, cores_out,
    work, zt, low, block, upper, inverse, col, oth,
    ztv, send1, recv1, send2, recv2, sendu, recvu, sendc, recvc, sendo, recvo,
):
    t = lax.axis_index("tile")
    l = lax.axis_index("layer")
    rows, order = diag_ref.shape[1], diag_ref.shape[2]
    panels = order // B
    span = cores_ref.shape[1]
    pair_base = t - t % 2
    mine = pl.ds(pl.multiple_of(l * rows, S), rows)
    first = t == 0
    even = t % 2 == 0

    def needed(j, piece):
        return (piece + 1) * rows > j * B

    def remote(src, dst, send, recv, to_t, to_l):
        return pltpu.make_async_remote_copy(
            src_ref=src, dst_ref=dst, send_sem=send, recv_sem=recv,
            device_id=(to_t, to_l), device_id_type=pl.DeviceIdType.MESH,
        )

    def down(j, half):
        return remote(
            diag_ref.at[0, :, pl.ds(pl.multiple_of(j * B, B), B)], work.at[j, mine, :],
            send1.at[half, j], recv1.at[j], 2 * half, l,
        )

    def kept(j):
        return pltpu.make_async_copy(
            diag_ref.at[0, :, pl.ds(pl.multiple_of(j * B, B), B)], work.at[j, mine, :], recv1.at[j]
        )

    def across(j, core, to_l):
        slot = work.at[j, mine, :]
        return remote(slot, slot, send2.at[j, core, to_l], recv2.at[j, l], pair_base + core, to_l)

    def landed(j, piece):
        slot = work.at[j, pl.ds(pl.multiple_of(piece * rows, S), rows), :]
        return remote(slot, slot, send2.at[j, 0, 0], recv2.at[j, piece], t, l)

    def basis_down(half):
        return remote(masked_t_ref, zt, sendu.at[half], recvu, 2 * half, l)

    def basis_kept():
        return pltpu.make_async_copy(masked_t_ref, zt, recvu)

    def basis_across():
        return remote(zt, zt, sendu.at[0], recvu, t + 1, l)

    def column_to(to_l):
        return remote(cores_ref.at[0, 0], col, sendc.at[to_l], recvc, t, to_l)

    def other_to(to_t):
        return remote(
            cores_ref.at[0, 0], oth.at[t % span], sendo.at[to_t], recvo.at[t % span], to_t, t // span
        )

    def each(count, act):
        lax.fori_loop(0, count, lambda i, c: (act(i), c)[1], 0)

    barrier = pltpu.get_barrier_semaphore()
    devices = tiles * layers
    me = t * layers + l

    def greet(i):
        d = lax.rem(me + 1 + i, devices)
        pl.semaphore_signal(
            barrier, inc=1, device_id=(d // layers, d % layers),
            device_id_type=pl.DeviceIdType.MESH,
        )

    @pl.when(first)
    def _():
        each(panels, lambda j: pl.when(needed(j, l))(lambda: kept(j).start()))
        basis_kept().start()

    each(devices - 1, greet)
    pl.semaphore_wait(barrier, devices - 1)

    def relay(j):
        @pl.when(even & needed(j, l))
        def _():
            @pl.when(first)
            def _():
                kept(j).wait()

            @pl.when(jnp.logical_not(first))
            def _():
                down(j, 0).wait_recv()

            def send(i):
                to_l = lax.rem(l + 1 + i, layers)
                across(j, 0, to_l).start()
                across(j, 1, to_l).start()

            across(j, 1, l).start()
            each(layers - 1, send)

    def arrive(j):
        def take(piece):
            @pl.when(needed(j, piece) & (jnp.logical_not(even) | (piece != l)))
            def _():
                landed(j, piece).wait_recv()

        each(layers, take)

    @pl.when(first)
    def _():
        def chunk(j):
            pl.when(needed(j, l))(
                lambda: each(tiles // 2 - 1, lambda h: down(j, tiles // 2 - 1 - h).start())
            )

        chunk(0)
        each(tiles // 2 - 1, lambda h: basis_down(tiles // 2 - 1 - h).start())
        each(panels - 1, lambda j: chunk(j + 1))

    relay(0)

    @pl.when(l == 0)
    def _():
        each(layers - 1, lambda i: column_to(i + 1).start())
        pltpu.make_async_copy(cores_ref.at[0, 0], col, recvc).start()

        def other(i):
            to_t = lax.rem(t + i, tiles)

            @pl.when((to_t != t) | (t // span != 0))
            def _():
                other_to(to_t).start()

        each(tiles, other)

        @pl.when(t // span == 0)
        def _():
            pltpu.make_async_copy(cores_ref.at[0, 0], oth.at[t % span], recvo.at[t % span]).start()

    def basis_relay():
        @pl.when(first)
        def _():
            basis_kept().wait()

        @pl.when(jnp.logical_not(first))
        def _():
            basis_down(0).wait_recv()

        @pl.when(even)
        def _():
            basis_across().start()

    low[...] = jnp.zeros_like(low)

    def panel(k, carry):
        at = pl.ds(pl.multiple_of(k * B, B), B)
        arrive(k)
        for c in range(panels):
            @pl.when(k == c)
            def _():
                here = slice(c * B, c * B + B)
                if c:
                    work2 = work[c, c * B :, :] - nt(low[c * B :, : c * B], low[here, : c * B])
                    low[c * B :, here] = work2
                else:
                    low[:, here] = work[0]
        block[...] = low[at, at]

        def midway():
            @pl.when(k + 1 < panels)
            def _():
                relay(k + 1)

        base_factor(block, upper, inverse, midway)
        low[at, at] = upper[...].T

        @pl.when(k == 0)
        def _():
            basis_relay()
            ztv[...] = zt[...]

        for c in range(panels):
            @pl.when(k == c)
            def _():
                here = slice(c * B, c * B + B)
                rest = slice(c * B + B, order)
                part = ztv[:, here]
                if c:
                    part = part - nt(ztv[:, : c * B], low[here, : c * B])
                ztv[:, here] = nt(part, inverse[...])
                if c + 1 < panels:
                    low[rest, here] = nt(low[rest, here], inverse[...])
        return carry

    lax.fori_loop(0, panels, panel, 0)

    factor_ref[0] = low[mine, :]
    z_ref[0] = ztv[...].T
    gram = nt(ztv[...], ztv[...])

    @pl.when(l == 0)
    def _():
        pltpu.make_async_copy(cores_ref.at[0, 0], col, recvc).wait()

    @pl.when(l != 0)
    def _():
        column_to(0).wait_recv()

    def take_other(s):
        local = (l == 0) & (l * span + s == t)

        @pl.when(local)
        def _():
            pltpu.make_async_copy(cores_ref.at[0, 0], oth.at[s], recvo.at[s]).wait()

        @pl.when(jnp.logical_not(local))
        def _():
            remote(cores_ref.at[0, 0], oth.at[s], sendo.at[0], recvo.at[s], t, l).wait_recv()

    each(span, take_other)
    coef = nn(col[...], gram)
    inner = nt(coef, col[...])
    inner = jnp.where(t > 0, inner, 0.0)
    partial = nn(masked_ref[0, mine, :], inner)
    diag_out[0] = diag_ref[0] - nt(partial, masked_ref[0])
    for s in range(span):
        other_id = l * span + s
        live = (t > other_id) & (other_id > 0)
        cores_out[0, s] = cores_ref[0, s] - jnp.where(live, nt(coef, oth[s]), 0.0)

    @pl.when(first)
    def _():
        def chunk(j):
            pl.when(needed(j, l))(lambda: each(tiles // 2 - 1, lambda h: down(j, h + 1).wait_send()))

        each(panels, chunk)
        each(tiles // 2 - 1, lambda h: basis_down(h + 1).wait_send())

    @pl.when(even)
    def _():
        basis_across().wait_send()

        def chunk(j):
            @pl.when(needed(j, l))
            def _():
                across(j, 1, l).wait_send()

                def sent(i):
                    to_l = lax.rem(l + 1 + i, layers)
                    across(j, 0, to_l).wait_send()
                    across(j, 1, to_l).wait_send()

                each(layers - 1, sent)

        each(panels, chunk)

    @pl.when(l == 0)
    def _():
        each(layers - 1, lambda i: column_to(i + 1).wait_send())

        def other(i):
            to_t = lax.rem(t + i, tiles)

            @pl.when((to_t != t) | (t // span != 0))
            def _():
                other_to(to_t).wait_send()

        each(tiles, other)


def body(tiles, layers, basis, ranks, cores, diag):
    rmax = basis.shape[2]
    span = cores.shape[1]
    rows, order = diag.shape[1], diag.shape[2]
    panels = order // B
    keep = (jnp.arange(rmax, dtype=jnp.int32)[None, :] < ranks[:, None]).astype(jnp.float32)
    masked = basis * keep[:, None, :]
    masked_t = masked[0].T
    vm = pl.BlockSpec(memory_space=pltpu.VMEM)
    f32 = jnp.float32
    dma = pltpu.SemaphoreType.DMA
    return pl.pallas_call(
        functools.partial(panel_kernel, tiles, layers),
        out_shape=(
            jax.ShapeDtypeStruct((1, rows, order), f32),
            jax.ShapeDtypeStruct((1, order, rmax), f32),
            jax.ShapeDtypeStruct(diag.shape, f32),
            jax.ShapeDtypeStruct(cores.shape, f32),
        ),
        in_specs=[vm] * 4,
        out_specs=(vm,) * 4,
        scratch_shapes=[
            pltpu.VMEM((panels, order, B), f32),
            pltpu.VMEM((rmax, order), f32),
            pltpu.VMEM((order, order), f32),
            pltpu.VMEM((B, B), f32),
            pltpu.VMEM((B, B), f32),
            pltpu.VMEM((B, B), f32),
            pltpu.VMEM((rmax, rmax), f32),
            pltpu.VMEM((span, rmax, rmax), f32),
            pltpu.VMEM((rmax, order), f32),
            dma((tiles // 2, panels)),
            dma((panels,)),
            dma((panels, 2, layers)),
            dma((panels, layers)),
            dma((tiles // 2,)),
            dma,
            dma((layers,)),
            dma,
            dma((tiles,)),
            dma((span,)),
        ],
        compiler_params=pltpu.CompilerParams(collective_id=0, has_side_effects=True),
    )(diag, masked, masked_t, cores)


def solution(mesh):
    placed = (
        P("tile", None, None),
        P("tile"),
        P("tile", "layer", None, None),
        P("tile", "layer", None),
    )
    return jax.shard_map(
        functools.partial(body, mesh.shape["tile"], mesh.shape["layer"]),
        mesh=mesh,
        in_specs=placed,
        out_specs=(
            P(None, "layer", None),
            P(),
            P("tile", "layer", None),
            P("tile", "layer", None, None),
        ),
        check_vma=False,
    )
```

```python
import functools

import jax
import jax.numpy as jnp
from jax import lax
from jax.experimental import pallas as pl
from jax.experimental.pallas import tpu as pltpu
from jax.sharding import PartitionSpec as P

HI = lax.Precision.HIGHEST
B = 128
S = 8


def nt(a, b):
    return lax.dot_general(
        a, b, (((1,), (1,)), ((), ())), precision=HI, preferred_element_type=jnp.float32
    )


def nn(a, b):
    return jnp.dot(a, b, precision=HI, preferred_element_type=jnp.float32)


def total(terms):
    while len(terms) > 1:
        terms = [
            terms[i] + terms[i + 1] if i + 1 < len(terms) else terms[i]
            for i in range(0, len(terms), 2)
        ]
    return terms[0]


def spread_lane(block, lane):
    return jnp.broadcast_to(block[:, lane : lane + 1], (S, B))


def pick_lane(block, lane):
    return jnp.take_along_axis(block, jnp.full((S, B), lane, jnp.int32), axis=1)


def spread_row(block, row):
    return jnp.broadcast_to(block[row : row + 1, :], (S, B))


def base_factor(tile_ref, upper_ref, inv_ref, midway):
    groups = B // S
    sub = lax.broadcasted_iota(jnp.int32, (S, B), 0)
    lane = lax.broadcasted_iota(jnp.int32, (S, B), 1)
    left = [tile_ref[S * g : S * g + S, :] for g in range(groups)]
    for b in range(groups):
        if b == groups // 2:
            midway()
        a = left[b]
        q = jnp.where(lane < S * b, a, jnp.where(lane == sub + S * b, 1.0, 0.0))
        cols = [pick_lane(a, S * b + j) for j in range(S)]
        e = [[spread_row(cols[j], i) if j <= i else None for j in range(S)] for i in range(S)]
        inv, low = [], [[None] * S for _ in range(S)]
        for j in range(S):
            inv.append(1.0 / e[j][j])
            for i in range(j + 1, S):
                low[i][j] = e[i][j] * inv[j]
            for k in range(j + 1, S):
                for i in range(k, S):
                    e[i][k] = e[i][k] - low[i][j] * e[k][j]
        ra = [spread_row(a, i) for i in range(S)]
        rq = [spread_row(q, i) for i in range(S)]
        for j in range(S):
            for i in range(j + 1, S):
                ra[i] = ra[i] - low[i][j] * ra[j]
                rq[i] = rq[i] - low[i][j] * rq[j]
        xa, xq = None, None
        for j in range(S):
            root = lax.rsqrt(e[j][j])
            ya, yq = ra[j] * root, rq[j] * root
            xa = ya if xa is None else jnp.where(sub == j, ya, xa)
            xq = yq if xq is None else jnp.where(sub == j, yq, xq)
        upper_ref[S * b : S * b + S, :] = jnp.where(lane >= sub + S * b, xa, 0.0)
        inv_ref[S * b : S * b + S, :] = xq
        if b + 1 == groups:
            break
        done = lane < S * b + S
        w = [jnp.where(done, rq[j], ra[j]) * inv[j] for j in range(S)]
        for i in range(S - 1, 0, -1):
            for j in range(i):
                w[j] = w[j] - low[i][j] * w[i]
        pivots = done & (lane >= S * b)
        for g in range(b + 1, groups):
            m = [spread_lane(left[g], S * b + j) for j in range(S)]
            left[g] = jnp.where(pivots, 0.0, left[g]) - total([m[j] * w[j] for j in range(S)])


def panel_kernel(
    tiles, layers, diag_ref, masked_ref, masked_t_ref, cores_ref,
    factor_ref, z_ref, diag_out, cores_out,
    work, zt, low, block, upper, inverse, col, oth,
    ztv, send1, recv1, send2, recv2, sendu, recvu, sendc, recvc, sendo, recvo,
):
    t = lax.axis_index("tile")
    l = lax.axis_index("layer")
    rows, order = diag_ref.shape[1], diag_ref.shape[2]
    panels = order // B
    span = cores_ref.shape[1]
    pair_base = t - t % 2
    mine = pl.ds(pl.multiple_of(l * rows, S), rows)
    first = t == 0
    even = t % 2 == 0

    def needed(j, piece):
        return (piece + 1) * rows > j * B

    def remote(src, dst, send, recv, to_t, to_l):
        return pltpu.make_async_remote_copy(
            src_ref=src, dst_ref=dst, send_sem=send, recv_sem=recv,
            device_id=(to_t, to_l), device_id_type=pl.DeviceIdType.MESH,
        )

    def down(j, half):
        return remote(
            diag_ref.at[0, :, pl.ds(pl.multiple_of(j * B, B), B)], work.at[j, mine, :],
            send1.at[half, j], recv1.at[j], 2 * half, l,
        )

    def kept(j):
        return pltpu.make_async_copy(
            diag_ref.at[0, :, pl.ds(pl.multiple_of(j * B, B), B)], work.at[j, mine, :], recv1.at[j]
        )

    def across(j, core, to_l):
        slot = work.at[j, mine, :]
        return remote(slot, slot, send2.at[j, core, to_l], recv2.at[j, l], pair_base + core, to_l)

    def landed(j, piece):
        slot = work.at[j, pl.ds(pl.multiple_of(piece * rows, S), rows), :]
        return remote(slot, slot, send2.at[j, 0, 0], recv2.at[j, piece], t, l)

    def basis_down(half):
        return remote(masked_t_ref, zt, sendu.at[half], recvu, 2 * half, l)

    def basis_kept():
        return pltpu.make_async_copy(masked_t_ref, zt, recvu)

    def basis_across():
        return remote(zt, zt, sendu.at[0], recvu, t + 1, l)

    def column_to(to_l):
        return remote(cores_ref.at[0, 0], col, sendc.at[to_l], recvc, t, to_l)

    def other_to(to_t):
        return remote(
            cores_ref.at[0, 0], oth.at[t % span], sendo.at[to_t], recvo.at[t % span], to_t, t // span
        )

    def each(count, act):
        lax.fori_loop(0, count, lambda i, c: (act(i), c)[1], 0)

    barrier = pltpu.get_barrier_semaphore()
    devices = tiles * layers
    me = t * layers + l

    def greet(i):
        d = lax.rem(me + 1 + i, devices)
        pl.semaphore_signal(
            barrier, inc=1, device_id=(d // layers, d % layers),
            device_id_type=pl.DeviceIdType.MESH,
        )

    @pl.when(first)
    def _():
        each(panels, lambda j: pl.when(needed(j, l))(lambda: kept(j).start()))
        basis_kept().start()

    each(devices - 1, greet)
    pl.semaphore_wait(barrier, devices - 1)

    def relay(j):
        @pl.when(even & needed(j, l))
        def _():
            @pl.when(first)
            def _():
                kept(j).wait()

            @pl.when(jnp.logical_not(first))
            def _():
                down(j, 0).wait_recv()

            def send(i):
                to_l = lax.rem(l + 1 + i, layers)
                across(j, 0, to_l).start()
                across(j, 1, to_l).start()

            across(j, 1, l).start()
            each(layers - 1, send)

    def arrive(j):
        def take(piece):
            @pl.when(needed(j, piece) & (jnp.logical_not(even) | (piece != l)))
            def _():
                landed(j, piece).wait_recv()

        each(layers, take)

    @pl.when(first)
    def _():
        def chunk(j):
            pl.when(needed(j, l))(
                lambda: each(tiles // 2 - 1, lambda h: down(j, tiles // 2 - 1 - h).start())
            )

        chunk(0)
        each(tiles // 2 - 1, lambda h: basis_down(tiles // 2 - 1 - h).start())
        each(panels - 1, lambda j: chunk(j + 1))

    relay(0)

    @pl.when(l == 0)
    def _():
        each(layers - 1, lambda i: column_to(i + 1).start())
        pltpu.make_async_copy(cores_ref.at[0, 0], col, recvc).start()

        def other(i):
            to_t = lax.rem(t + i, tiles)

            @pl.when((to_t != t) | (t // span != 0))
            def _():
                other_to(to_t).start()

        each(tiles, other)

        @pl.when(t // span == 0)
        def _():
            pltpu.make_async_copy(cores_ref.at[0, 0], oth.at[t % span], recvo.at[t % span]).start()

    def basis_relay():
        @pl.when(first)
        def _():
            basis_kept().wait()

        @pl.when(jnp.logical_not(first))
        def _():
            basis_down(0).wait_recv()

        @pl.when(even)
        def _():
            basis_across().start()

    low[...] = jnp.zeros_like(low)

    def panel(k, carry):
        at = pl.ds(pl.multiple_of(k * B, B), B)
        arrive(k)
        for c in range(panels):
            @pl.when(k == c)
            def _():
                here = slice(c * B, c * B + B)
                if c:
                    work2 = work[c, c * B :, :] - nt(low[c * B :, : c * B], low[here, : c * B])
                    low[c * B :, here] = work2
                else:
                    low[:, here] = work[0]
        block[...] = low[at, at]

        def midway():
            @pl.when(k + 1 < panels)
            def _():
                relay(k + 1)

        base_factor(block, upper, inverse, midway)
        low[at, at] = upper[...].T

        @pl.when(k == 0)
        def _():
            basis_relay()
            ztv[...] = zt[...]

        for c in range(panels):
            @pl.when(k == c)
            def _():
                here = slice(c * B, c * B + B)
                rest = slice(c * B + B, order)
                part = ztv[:, here]
                if c:
                    part = part - nt(ztv[:, : c * B], low[here, : c * B])
                ztv[:, here] = nt(part, inverse[...])
                if c + 1 < panels:
                    low[rest, here] = nt(low[rest, here], inverse[...])
        return carry

    lax.fori_loop(0, panels, panel, 0)

    factor_ref[0] = low[mine, :]
    z_ref[0] = ztv[...].T
    gram = nt(ztv[...], ztv[...])

    @pl.when(l == 0)
    def _():
        pltpu.make_async_copy(cores_ref.at[0, 0], col, recvc).wait()

    @pl.when(l != 0)
    def _():
        column_to(0).wait_recv()

    def take_other(s):
        local = (l == 0) & (l * span + s == t)

        @pl.when(local)
        def _():
            pltpu.make_async_copy(cores_ref.at[0, 0], oth.at[s], recvo.at[s]).wait()

        @pl.when(jnp.logical_not(local))
        def _():
            remote(cores_ref.at[0, 0], oth.at[s], sendo.at[0], recvo.at[s], t, l).wait_recv()

    each(span, take_other)
    coef = nn(col[...], gram)
    inner = nt(coef, col[...])
    inner = jnp.where(t > 0, inner, 0.0)
    partial = nn(masked_ref[0, mine, :], inner)
    diag_out[0] = diag_ref[0] - nt(partial, masked_ref[0])
    for s in range(span):
        other_id = l * span + s
        live = (t > other_id) & (other_id > 0)
        cores_out[0, s] = cores_ref[0, s] - jnp.where(live, nt(coef, oth[s]), 0.0)

    @pl.when(first)
    def _():
        def chunk(j):
            pl.when(needed(j, l))(lambda: each(tiles // 2 - 1, lambda h: down(j, h + 1).wait_send()))

        each(panels, chunk)
        each(tiles // 2 - 1, lambda h: basis_down(h + 1).wait_send())

    @pl.when(even)
    def _():
        basis_across().wait_send()

        def chunk(j):
            @pl.when(needed(j, l))
            def _():
                across(j, 1, l).wait_send()

                def sent(i):
                    to_l = lax.rem(l + 1 + i, layers)
                    across(j, 0, to_l).wait_send()
                    across(j, 1, to_l).wait_send()

                each(layers - 1, sent)

        each(panels, chunk)

    @pl.when(l == 0)
    def _():
        each(layers - 1, lambda i: column_to(i + 1).wait_send())

        def other(i):
            to_t = lax.rem(t + i, tiles)

            @pl.when((to_t != t) | (t // span != 0))
            def _():
                other_to(to_t).wait_send()

        each(tiles, other)


def body(tiles, layers, basis, ranks, cores, diag):
    rmax = basis.shape[2]
    span = cores.shape[1]
    rows, order = diag.shape[1], diag.shape[2]
    panels = order // B
    keep = (jnp.arange(rmax, dtype=jnp.int32)[None, :] < ranks[:, None]).astype(jnp.float32)
    masked = basis * keep[:, None, :]
    masked_t = masked[0].T
    vm = pl.BlockSpec(memory_space=pltpu.VMEM)
    f32 = jnp.float32
    dma = pltpu.SemaphoreType.DMA
    return pl.pallas_call(
        functools.partial(panel_kernel, tiles, layers),
        out_shape=(
            jax.ShapeDtypeStruct((1, rows, order), f32),
            jax.ShapeDtypeStruct((1, order, rmax), f32),
            jax.ShapeDtypeStruct(diag.shape, f32),
            jax.ShapeDtypeStruct(cores.shape, f32),
        ),
        in_specs=[vm] * 4,
        out_specs=(vm,) * 4,
        scratch_shapes=[
            pltpu.VMEM((panels, order, B), f32),
            pltpu.VMEM((rmax, order), f32),
            pltpu.VMEM((order, order), f32),
            pltpu.VMEM((B, B), f32),
            pltpu.VMEM((B, B), f32),
            pltpu.VMEM((B, B), f32),
            pltpu.VMEM((rmax, rmax), f32),
            pltpu.VMEM((span, rmax, rmax), f32),
            pltpu.VMEM((rmax, order), f32),
            dma((tiles // 2, panels)),
            dma((panels,)),
            dma((panels, 2, layers)),
            dma((panels, layers)),
            dma((tiles // 2,)),
            dma,
            dma((layers,)),
            dma,
            dma((tiles,)),
            dma((span,)),
        ],
        compiler_params=pltpu.CompilerParams(collective_id=0, has_side_effects=True),
    )(diag, masked, masked_t, cores)


def solution(mesh):
    placed = (
        P("tile", None, None),
        P("tile"),
        P("tile", "layer", None, None),
        P("tile", "layer", None),
    )
    return jax.shard_map(
        functools.partial(body, mesh.shape["tile"], mesh.shape["layer"]),
        mesh=mesh,
        in_specs=placed,
        out_specs=(
            P(None, "layer", None),
            P(),
            P("tile", "layer", None),
            P("tile", "layer", None, None),
        ),
        check_vma=False,
    )
```

```python
import functools

import jax
import jax.numpy as jnp
from jax import lax
from jax.experimental import pallas as pl
from jax.experimental.pallas import tpu as pltpu
from jax.sharding import PartitionSpec as P

HI = lax.Precision.HIGHEST
B = 128
S = 8
NEAR = 2


def nt(a, b):
    return lax.dot_general(
        a, b, (((1,), (1,)), ((), ())), precision=HI, preferred_element_type=jnp.float32
    )


def nn(a, b):
    return jnp.dot(a, b, precision=HI, preferred_element_type=jnp.float32)


def split(a):
    high = a.astype(jnp.bfloat16)
    return high, (a - high.astype(jnp.float32)).astype(jnp.bfloat16)


def nn3(a, b):
    ah, al = split(a)
    bh, bl = split(b)
    dot = functools.partial(jnp.dot, preferred_element_type=jnp.float32)
    return dot(ah, bh) + (dot(ah, bl) + dot(al, bh))


def total(terms):
    while len(terms) > 1:
        terms = [
            terms[i] + terms[i + 1] if i + 1 < len(terms) else terms[i]
            for i in range(0, len(terms), 2)
        ]
    return terms[0]


def spread_lane(block, lane):
    return jnp.broadcast_to(block[:, lane : lane + 1], (S, B))


def pick_lane(block, lane):
    return jnp.take_along_axis(block, jnp.full((S, B), lane, jnp.int32), axis=1)


def spread_row(block, row):
    return jnp.broadcast_to(block[row : row + 1, :], (S, B))


def base_factor(tile_ref, upper_ref, inv_ref):
    groups = B // S
    sub = lax.broadcasted_iota(jnp.int32, (S, B), 0)
    lane = lax.broadcasted_iota(jnp.int32, (S, B), 1)
    left = [tile_ref[S * g : S * g + S, :] for g in range(groups)]
    for b in range(groups):
        a = left[b]
        q = jnp.where(lane < S * b, a, jnp.where(lane == sub + S * b, 1.0, 0.0))
        cols = [pick_lane(a, S * b + j) for j in range(S)]
        e = [[spread_row(cols[j], i) if j <= i else None for j in range(S)] for i in range(S)]
        inv, low = [], [[None] * S for _ in range(S)]
        for j in range(S):
            inv.append(1.0 / e[j][j])
            for i in range(j + 1, S):
                low[i][j] = e[i][j] * inv[j]
            for k in range(j + 1, S):
                for i in range(k, S):
                    e[i][k] = e[i][k] - low[i][j] * e[k][j]
        ra = [spread_row(a, i) for i in range(S)]
        rq = [spread_row(q, i) for i in range(S)]
        for j in range(S):
            for i in range(j + 1, S):
                ra[i] = ra[i] - low[i][j] * ra[j]
                rq[i] = rq[i] - low[i][j] * rq[j]
        xa, xq = None, None
        for j in range(S):
            root = lax.rsqrt(e[j][j])
            ya, yq = ra[j] * root, rq[j] * root
            xa = ya if xa is None else jnp.where(sub == j, ya, xa)
            xq = yq if xq is None else jnp.where(sub == j, yq, xq)
        upper_ref[S * b : S * b + S, :] = jnp.where(lane >= sub + S * b, xa, 0.0)
        inv_ref[S * b : S * b + S, :] = xq
        if b + 1 == groups:
            break
        done = lane < S * b + S
        w = [jnp.where(done, rq[j], ra[j]) * inv[j] for j in range(S)]
        for i in range(S - 1, 0, -1):
            for j in range(i):
                w[j] = w[j] - low[i][j] * w[i]
        pivots = done & (lane >= S * b)
        for g in range(b + 1, min(b + 1 + NEAR, groups)):
            m = [spread_lane(left[g], S * b + j) for j in range(S)]
            left[g] = jnp.where(pivots, 0.0, left[g]) - total([m[j] * w[j] for j in range(S)])
        far = b + 1 + NEAR
        if far < groups:
            packed = w[0]
            for j in range(1, S):
                packed = jnp.where(sub == j, w[j], packed)
            rows = [packed if g == b else jnp.zeros((S, B), jnp.float32) for g in range(groups)]
            moved = nn3(jnp.concatenate(left[far:], axis=0), jnp.concatenate(rows, axis=0))
            for g in range(far, groups):
                at = S * (g - far)
                left[g] = jnp.where(pivots, 0.0, left[g]) - moved[at : at + S, :]


def panel_kernel(
    tiles, layers, diag_ref, masked_ref, masked_t_ref, cores_ref,
    factor_ref, z_ref, diag_out, cores_out,
    work, zt, low, block, upper, inverse, col, oth,
    ztv, send1, recv1, send2, recv2, sendu, recvu, sendc, recvc, sendo, recvo,
):
    t = lax.axis_index("tile")
    l = lax.axis_index("layer")
    rows, order = diag_ref.shape[1], diag_ref.shape[2]
    panels = order // B
    span = cores_ref.shape[1]
    pair_base = t - t % 2
    mine = pl.ds(pl.multiple_of(l * rows, S), rows)
    first = t == 0
    even = t % 2 == 0

    def needed(j, piece):
        return (piece + 1) * rows > j * B

    def remote(src, dst, send, recv, to_t, to_l):
        return pltpu.make_async_remote_copy(
            src_ref=src, dst_ref=dst, send_sem=send, recv_sem=recv,
            device_id=(to_t, to_l), device_id_type=pl.DeviceIdType.MESH,
        )

    def down(j, half):
        return remote(
            diag_ref.at[0, :, pl.ds(pl.multiple_of(j * B, B), B)], work.at[j, mine, :],
            send1.at[half, j], recv1.at[j], 2 * half, l,
        )

    def kept(j):
        return pltpu.make_async_copy(
            diag_ref.at[0, :, pl.ds(pl.multiple_of(j * B, B), B)], work.at[j, mine, :], recv1.at[j]
        )

    def across(j, core, to_l):
        slot = work.at[j, mine, :]
        return remote(slot, slot, send2.at[j, core, to_l], recv2.at[j, l], pair_base + core, to_l)

    def landed(j, piece):
        slot = work.at[j, pl.ds(pl.multiple_of(piece * rows, S), rows), :]
        return remote(slot, slot, send2.at[j, 0, 0], recv2.at[j, piece], t, l)

    def basis_down(half):
        return remote(masked_t_ref, zt, sendu.at[half], recvu, 2 * half, l)

    def basis_kept():
        return pltpu.make_async_copy(masked_t_ref, zt, recvu)

    def basis_across():
        return remote(zt, zt, sendu.at[0], recvu, t + 1, l)

    def column_to(to_l):
        return remote(cores_ref.at[0, 0], col, sendc.at[to_l], recvc, t, to_l)

    def other_to(to_t):
        return remote(
            cores_ref.at[0, 0], oth.at[t % span], sendo.at[to_t], recvo.at[t % span], to_t, t // span
        )

    def each(count, act):
        lax.fori_loop(0, count, lambda i, c: (act(i), c)[1], 0)

    barrier = pltpu.get_barrier_semaphore()
    devices = tiles * layers
    me = t * layers + l

    def greet(i):
        d = lax.rem(me + 1 + i, devices)
        pl.semaphore_signal(
            barrier, inc=1, device_id=(d // layers, d % layers),
            device_id_type=pl.DeviceIdType.MESH,
        )

    @pl.when(first)
    def _():
        each(panels, lambda j: pl.when(needed(j, l))(lambda: kept(j).start()))
        basis_kept().start()

    each(devices - 1, greet)
    pl.semaphore_wait(barrier, devices - 1)

    def relay(j):
        @pl.when(even & needed(j, l))
        def _():
            @pl.when(first)
            def _():
                kept(j).wait()

            @pl.when(jnp.logical_not(first))
            def _():
                down(j, 0).wait_recv()

            def send(i):
                to_l = lax.rem(l + 1 + i, layers)
                across(j, 0, to_l).start()
                across(j, 1, to_l).start()

            across(j, 1, l).start()
            each(layers - 1, send)

    def arrive(j):
        def take(piece):
            @pl.when(needed(j, piece) & (jnp.logical_not(even) | (piece != l)))
            def _():
                landed(j, piece).wait_recv()

        each(layers, take)

    @pl.when(first)
    def _():
        def chunk(j):
            pl.when(needed(j, l))(
                lambda: each(tiles // 2 - 1, lambda h: down(j, tiles // 2 - 1 - h).start())
            )

        chunk(0)
        if panels > 1:
            chunk(1)
        each(tiles // 2 - 1, lambda h: basis_down(tiles // 2 - 1 - h).start())
        each(panels - 2, lambda j: chunk(j + 2))

    relay(0)

    @pl.when(l == 0)
    def _():
        each(layers - 1, lambda i: column_to(i + 1).start())
        pltpu.make_async_copy(cores_ref.at[0, 0], col, recvc).start()

        def other(i):
            to_t = lax.rem(t + i, tiles)

            @pl.when((to_t != t) | (t // span != 0))
            def _():
                other_to(to_t).start()

        each(tiles, other)

        @pl.when(t // span == 0)
        def _():
            pltpu.make_async_copy(cores_ref.at[0, 0], oth.at[t % span], recvo.at[t % span]).start()

    def basis_relay():
        @pl.when(first)
        def _():
            basis_kept().wait()

        @pl.when(jnp.logical_not(first))
        def _():
            basis_down(0).wait_recv()

        @pl.when(even)
        def _():
            basis_across().start()

    low[...] = jnp.zeros_like(low)

    def panel(k, carry):
        at = pl.ds(pl.multiple_of(k * B, B), B)
        arrive(k)

        @pl.when(k + 1 < panels)
        def _():
            relay(k + 1)

        for c in range(panels):
            @pl.when(k == c)
            def _():
                here = slice(c * B, c * B + B)
                if c:
                    work2 = work[c, c * B :, :] - nt(low[c * B :, : c * B], low[here, : c * B])
                    low[c * B :, here] = work2
                else:
                    low[:, here] = work[0]
        block[...] = low[at, at]

        base_factor(block, upper, inverse)
        low[at, at] = upper[...].T

        @pl.when(k == 0)
        def _():
            basis_relay()
            ztv[...] = zt[...]

        for c in range(panels):
            @pl.when(k == c)
            def _():
                here = slice(c * B, c * B + B)
                rest = slice(c * B + B, order)
                part = ztv[:, here]
                if c:
                    part = part - nt(ztv[:, : c * B], low[here, : c * B])
                ztv[:, here] = nt(part, inverse[...])
                if c + 1 < panels:
                    low[rest, here] = nt(low[rest, here], inverse[...])
        return carry

    lax.fori_loop(0, panels, panel, 0)

    factor_ref[0] = low[mine, :]
    z_ref[0] = ztv[...].T
    gram = nt(ztv[...], ztv[...])

    @pl.when(l == 0)
    def _():
        pltpu.make_async_copy(cores_ref.at[0, 0], col, recvc).wait()

    @pl.when(l != 0)
    def _():
        column_to(0).wait_recv()

    def take_other(s):
        local = (l == 0) & (l * span + s == t)

        @pl.when(local)
        def _():
            pltpu.make_async_copy(cores_ref.at[0, 0], oth.at[s], recvo.at[s]).wait()

        @pl.when(jnp.logical_not(local))
        def _():
            remote(cores_ref.at[0, 0], oth.at[s], sendo.at[0], recvo.at[s], t, l).wait_recv()

    each(span, take_other)
    coef = nn(col[...], gram)
    inner = nt(coef, col[...])
    inner = jnp.where(t > 0, inner, 0.0)
    partial = nn(masked_ref[0, mine, :], inner)
    diag_out[0] = diag_ref[0] - nt(partial, masked_ref[0])
    for s in range(span):
        other_id = l * span + s
        live = (t > other_id) & (other_id > 0)
        cores_out[0, s] = cores_ref[0, s] - jnp.where(live, nt(coef, oth[s]), 0.0)

    @pl.when(first)
    def _():
        def chunk(j):
            pl.when(needed(j, l))(lambda: each(tiles // 2 - 1, lambda h: down(j, h + 1).wait_send()))

        each(panels, chunk)
        each(tiles // 2 - 1, lambda h: basis_down(h + 1).wait_send())

    @pl.when(even)
    def _():
        basis_across().wait_send()

        def chunk(j):
            @pl.when(needed(j, l))
            def _():
                across(j, 1, l).wait_send()

                def sent(i):
                    to_l = lax.rem(l + 1 + i, layers)
                    across(j, 0, to_l).wait_send()
                    across(j, 1, to_l).wait_send()

                each(layers - 1, sent)

        each(panels, chunk)

    @pl.when(l == 0)
    def _():
        each(layers - 1, lambda i: column_to(i + 1).wait_send())

        def other(i):
            to_t = lax.rem(t + i, tiles)

            @pl.when((to_t != t) | (t // span != 0))
            def _():
                other_to(to_t).wait_send()

        each(tiles, other)


def body(tiles, layers, basis, ranks, cores, diag):
    rmax = basis.shape[2]
    span = cores.shape[1]
    rows, order = diag.shape[1], diag.shape[2]
    panels = order // B
    keep = (jnp.arange(rmax, dtype=jnp.int32)[None, :] < ranks[:, None]).astype(jnp.float32)
    masked = basis * keep[:, None, :]
    masked_t = masked[0].T
    vm = pl.BlockSpec(memory_space=pltpu.VMEM)
    f32 = jnp.float32
    dma = pltpu.SemaphoreType.DMA
    return pl.pallas_call(
        functools.partial(panel_kernel, tiles, layers),
        out_shape=(
            jax.ShapeDtypeStruct((1, rows, order), f32),
            jax.ShapeDtypeStruct((1, order, rmax), f32),
            jax.ShapeDtypeStruct(diag.shape, f32),
            jax.ShapeDtypeStruct(cores.shape, f32),
        ),
        in_specs=[vm] * 4,
        out_specs=(vm,) * 4,
        scratch_shapes=[
            pltpu.VMEM((panels, order, B), f32),
            pltpu.VMEM((rmax, order), f32),
            pltpu.VMEM((order, order), f32),
            pltpu.VMEM((B, B), f32),
            pltpu.VMEM((B, B), f32),
            pltpu.VMEM((B, B), f32),
            pltpu.VMEM((rmax, rmax), f32),
            pltpu.VMEM((span, rmax, rmax), f32),
            pltpu.VMEM((rmax, order), f32),
            dma((tiles // 2, panels)),
            dma((panels,)),
            dma((panels, 2, layers)),
            dma((panels, layers)),
            dma((tiles // 2,)),
            dma,
            dma((layers,)),
            dma,
            dma((tiles,)),
            dma((span,)),
        ],
        compiler_params=pltpu.CompilerParams(collective_id=0, has_side_effects=True),
    )(diag, masked, masked_t, cores)


def solution(mesh):
    placed = (
        P("tile", None, None),
        P("tile"),
        P("tile", "layer", None, None),
        P("tile", "layer", None),
    )
    return jax.shard_map(
        functools.partial(body, mesh.shape["tile"], mesh.shape["layer"]),
        mesh=mesh,
        in_specs=placed,
        out_specs=(
            P(None, "layer", None),
            P(),
            P("tile", "layer", None),
            P("tile", "layer", None, None),
        ),
        check_vma=False,
    )
```

```python
import functools

import jax
import jax.numpy as jnp
from jax import lax
from jax.experimental import pallas as pl
from jax.experimental.pallas import tpu as pltpu
from jax.sharding import PartitionSpec as P

B = 128
S = 8
NEAR = 2


def split(a):
    high = a.astype(jnp.bfloat16)
    return high, (a - high.astype(jnp.float32)).astype(jnp.bfloat16)


def three(a, b, dims):
    ah, al = split(a)
    bh, bl = split(b)
    dot = functools.partial(
        lax.dot_general, dimension_numbers=(dims, ((), ())), preferred_element_type=jnp.float32
    )
    return dot(ah, bh) + (dot(ah, bl) + dot(al, bh))


def nt(a, b):
    return three(a, b, ((1,), (1,)))


def nn(a, b):
    return three(a, b, ((1,), (0,)))


def total(terms):
    while len(terms) > 1:
        terms = [
            terms[i] + terms[i + 1] if i + 1 < len(terms) else terms[i]
            for i in range(0, len(terms), 2)
        ]
    return terms[0]


def spread_lane(block, lane):
    return jnp.broadcast_to(block[:, lane : lane + 1], (S, B))


def pick_lane(block, lane):
    return jnp.take_along_axis(block, jnp.full((S, B), lane, jnp.int32), axis=1)


def spread_row(block, row):
    return jnp.broadcast_to(block[row : row + 1, :], (S, B))


def base_factor(tile_ref, upper_ref, inv_ref):
    groups = B // S
    sub = lax.broadcasted_iota(jnp.int32, (S, B), 0)
    lane = lax.broadcasted_iota(jnp.int32, (S, B), 1)
    left = [tile_ref[S * g : S * g + S, :] for g in range(groups)]
    for b in range(groups):
        a = left[b]
        q = jnp.where(lane < S * b, a, jnp.where(lane == sub + S * b, 1.0, 0.0))
        cols = [pick_lane(a, S * b + j) for j in range(S)]
        e = [[spread_row(cols[j], i) if j <= i else None for j in range(S)] for i in range(S)]
        inv, low = [], [[None] * S for _ in range(S)]
        for j in range(S):
            inv.append(1.0 / e[j][j])
            for i in range(j + 1, S):
                low[i][j] = e[i][j] * inv[j]
            for k in range(j + 1, S):
                for i in range(k, S):
                    e[i][k] = e[i][k] - low[i][j] * e[k][j]
        ra = [spread_row(a, i) for i in range(S)]
        rq = [spread_row(q, i) for i in range(S)]
        for j in range(S):
            for i in range(j + 1, S):
                ra[i] = ra[i] - low[i][j] * ra[j]
                rq[i] = rq[i] - low[i][j] * rq[j]
        xa, xq = None, None
        for j in range(S):
            root = lax.rsqrt(e[j][j])
            ya, yq = ra[j] * root, rq[j] * root
            xa = ya if xa is None else jnp.where(sub == j, ya, xa)
            xq = yq if xq is None else jnp.where(sub == j, yq, xq)
        upper_ref[S * b : S * b + S, :] = jnp.where(lane >= sub + S * b, xa, 0.0)
        inv_ref[S * b : S * b + S, :] = xq
        if b + 1 == groups:
            break
        done = lane < S * b + S
        w = [jnp.where(done, rq[j], ra[j]) * inv[j] for j in range(S)]
        for i in range(S - 1, 0, -1):
            for j in range(i):
                w[j] = w[j] - low[i][j] * w[i]
        pivots = done & (lane >= S * b)
        for g in range(b + 1, min(b + 1 + NEAR, groups)):
            m = [spread_lane(left[g], S * b + j) for j in range(S)]
            left[g] = jnp.where(pivots, 0.0, left[g]) - total([m[j] * w[j] for j in range(S)])
        far = b + 1 + NEAR
        if far < groups:
            packed = w[0]
            for j in range(1, S):
                packed = jnp.where(sub == j, w[j], packed)
            rows = [packed if g == b else jnp.zeros((S, B), jnp.float32) for g in range(groups)]
            moved = nn(jnp.concatenate(left[far:], axis=0), jnp.concatenate(rows, axis=0))
            for g in range(far, groups):
                at = S * (g - far)
                left[g] = jnp.where(pivots, 0.0, left[g]) - moved[at : at + S, :]


def panel_kernel(
    tiles, layers, diag_ref, masked_t_ref, cores_ref,
    factor_ref, z_ref, diag_out, cores_out,
    work, zt, low, block, upper, inverse, col, oth,
    ztv, own_rows, send1, recv1, send2, recv2, sendu, recvu, sendc, recvc, sendo, recvo,
):
    t = lax.axis_index("tile")
    l = lax.axis_index("layer")
    rows, order = diag_ref.shape[1], diag_ref.shape[2]
    panels = order // B
    span = cores_ref.shape[1]
    pair_base = t - t % 2
    mine = pl.ds(pl.multiple_of(l * rows, S), rows)
    first = t == 0
    even = t % 2 == 0

    def needed(j, piece):
        return (piece + 1) * rows > j * B

    def remote(src, dst, send, recv, to_t, to_l):
        return pltpu.make_async_remote_copy(
            src_ref=src, dst_ref=dst, send_sem=send, recv_sem=recv,
            device_id=(to_t, to_l), device_id_type=pl.DeviceIdType.MESH,
        )

    def down(j, half):
        return remote(
            diag_ref.at[0, :, pl.ds(pl.multiple_of(j * B, B), B)], work.at[j, mine, :],
            send1.at[half, j], recv1.at[j], 2 * half, l,
        )

    def kept(j):
        return pltpu.make_async_copy(
            diag_ref.at[0, :, pl.ds(pl.multiple_of(j * B, B), B)], work.at[j, mine, :], recv1.at[j]
        )

    def across(j, core, to_l):
        slot = work.at[j, mine, :]
        return remote(slot, slot, send2.at[j, core, to_l], recv2.at[j, l], pair_base + core, to_l)

    def landed(j, piece):
        slot = work.at[j, pl.ds(pl.multiple_of(piece * rows, S), rows), :]
        return remote(slot, slot, send2.at[j, 0, 0], recv2.at[j, piece], t, l)

    def basis_down(half):
        return remote(masked_t_ref, zt, sendu.at[half], recvu, 2 * half, l)

    def basis_kept():
        return pltpu.make_async_copy(masked_t_ref, zt, recvu)

    def basis_across():
        return remote(zt, zt, sendu.at[0], recvu, t + 1, l)

    def column_to(to_l):
        return remote(cores_ref.at[0, 0], col, sendc.at[to_l], recvc, t, to_l)

    def other_to(to_t):
        return remote(
            cores_ref.at[0, 0], oth.at[t % span], sendo.at[to_t], recvo.at[t % span], to_t, t // span
        )

    def each(count, act):
        lax.fori_loop(0, count, lambda i, c: (act(i), c)[1], 0)

    barrier = pltpu.get_barrier_semaphore()
    devices = tiles * layers
    me = t * layers + l

    def greet(i):
        d = lax.rem(me + 1 + i, devices)
        pl.semaphore_signal(
            barrier, inc=1, device_id=(d // layers, d % layers),
            device_id_type=pl.DeviceIdType.MESH,
        )

    @pl.when(first)
    def _():
        each(panels, lambda j: pl.when(needed(j, l))(lambda: kept(j).start()))
        basis_kept().start()

    each(devices - 1, greet)
    pl.semaphore_wait(barrier, devices - 1)

    def relay(j):
        @pl.when(even & needed(j, l))
        def _():
            @pl.when(first)
            def _():
                kept(j).wait()

            @pl.when(jnp.logical_not(first))
            def _():
                down(j, 0).wait_recv()

            def send(i):
                to_l = lax.rem(l + 1 + i, layers)
                across(j, 0, to_l).start()
                across(j, 1, to_l).start()

            across(j, 1, l).start()
            each(layers - 1, send)

    def arrive(j):
        def take(piece):
            @pl.when(needed(j, piece) & (jnp.logical_not(even) | (piece != l)))
            def _():
                landed(j, piece).wait_recv()

        each(layers, take)

    @pl.when(first)
    def _():
        def chunk(j):
            pl.when(needed(j, l))(
                lambda: each(tiles // 2 - 1, lambda h: down(j, tiles // 2 - 1 - h).start())
            )

        chunk(0)
        if panels > 1:
            chunk(1)
        each(tiles // 2 - 1, lambda h: basis_down(tiles // 2 - 1 - h).start())
        each(panels - 2, lambda j: chunk(j + 2))

    relay(0)

    @pl.when(l == 0)
    def _():
        each(layers - 1, lambda i: column_to(i + 1).start())
        pltpu.make_async_copy(cores_ref.at[0, 0], col, recvc).start()

        def other(i):
            to_t = lax.rem(t + i, tiles)

            @pl.when((to_t != t) | (t // span != 0))
            def _():
                other_to(to_t).start()

        each(tiles, other)

        @pl.when(t // span == 0)
        def _():
            pltpu.make_async_copy(cores_ref.at[0, 0], oth.at[t % span], recvo.at[t % span]).start()

    def basis_relay():
        @pl.when(first)
        def _():
            basis_kept().wait()

        @pl.when(jnp.logical_not(first))
        def _():
            basis_down(0).wait_recv()

        @pl.when(even)
        def _():
            basis_across().start()

    low[...] = jnp.zeros_like(low)
    own_rows[...] = masked_t_ref[...].T

    def panel(k, carry):
        at = pl.ds(pl.multiple_of(k * B, B), B)
        arrive(k)

        @pl.when(k + 1 < panels)
        def _():
            relay(k + 1)

        for c in range(panels):
            @pl.when(k == c)
            def _():
                here = slice(c * B, c * B + B)
                if c:
                    work2 = work[c, c * B :, :] - nt(low[c * B :, : c * B], low[here, : c * B])
                    low[c * B :, here] = work2
                else:
                    low[:, here] = work[0]
        block[...] = low[at, at]

        base_factor(block, upper, inverse)
        low[at, at] = upper[...].T

        @pl.when(k == 0)
        def _():
            basis_relay()
            ztv[...] = zt[...]

        for c in range(panels):
            @pl.when(k == c)
            def _():
                here = slice(c * B, c * B + B)
                rest = slice(c * B + B, order)
                part = ztv[:, here]
                if c:
                    part = part - nt(ztv[:, : c * B], low[here, : c * B])
                ztv[:, here] = nt(part, inverse[...])
                if c + 1 < panels:
                    low[rest, here] = nt(low[rest, here], inverse[...])
        return carry

    lax.fori_loop(0, panels, panel, 0)

    factor_ref[0] = low[mine, :]
    z_ref[...] = ztv[...]
    gram = nt(ztv[...], ztv[...])

    @pl.when(l == 0)
    def _():
        pltpu.make_async_copy(cores_ref.at[0, 0], col, recvc).wait()

    @pl.when(l != 0)
    def _():
        column_to(0).wait_recv()

    def take_other(s):
        local = (l == 0) & (l * span + s == t)

        @pl.when(local)
        def _():
            pltpu.make_async_copy(cores_ref.at[0, 0], oth.at[s], recvo.at[s]).wait()

        @pl.when(jnp.logical_not(local))
        def _():
            remote(cores_ref.at[0, 0], oth.at[s], sendo.at[0], recvo.at[s], t, l).wait_recv()

    each(span, take_other)
    coef = nn(col[...], gram)
    inner = nt(coef, col[...])
    inner = jnp.where(t > 0, inner, 0.0)
    partial = nn(own_rows[mine, :], inner)
    diag_out[0] = diag_ref[0] - nn(partial, masked_t_ref[...])
    for s in range(span):
        other_id = l * span + s
        live = (t > other_id) & (other_id > 0)
        cores_out[0, s] = cores_ref[0, s] - jnp.where(live, nt(coef, oth[s]), 0.0)

    @pl.when(first)
    def _():
        def chunk(j):
            pl.when(needed(j, l))(lambda: each(tiles // 2 - 1, lambda h: down(j, h + 1).wait_send()))

        each(panels, chunk)
        each(tiles // 2 - 1, lambda h: basis_down(h + 1).wait_send())

    @pl.when(even)
    def _():
        basis_across().wait_send()

        def chunk(j):
            @pl.when(needed(j, l))
            def _():
                across(j, 1, l).wait_send()

                def sent(i):
                    to_l = lax.rem(l + 1 + i, layers)
                    across(j, 0, to_l).wait_send()
                    across(j, 1, to_l).wait_send()

                each(layers - 1, sent)

        each(panels, chunk)

    @pl.when(l == 0)
    def _():
        each(layers - 1, lambda i: column_to(i + 1).wait_send())

        def other(i):
            to_t = lax.rem(t + i, tiles)

            @pl.when((to_t != t) | (t // span != 0))
            def _():
                other_to(to_t).wait_send()

        each(tiles, other)


def body(tiles, layers, basis, ranks, cores, diag):
    rmax = basis.shape[2]
    span = cores.shape[1]
    rows, order = diag.shape[1], diag.shape[2]
    panels = order // B
    keep = (jnp.arange(rmax, dtype=jnp.int32)[None, :] < ranks[:, None]).astype(jnp.float32)
    masked = basis * keep[:, None, :]
    masked_t = masked[0].T
    vm = pl.BlockSpec(memory_space=pltpu.VMEM)
    f32 = jnp.float32
    dma = pltpu.SemaphoreType.DMA
    factors, zt, schur, couplings = pl.pallas_call(
        functools.partial(panel_kernel, tiles, layers),
        out_shape=(
            jax.ShapeDtypeStruct((1, rows, order), f32),
            jax.ShapeDtypeStruct((rmax, order), f32),
            jax.ShapeDtypeStruct(diag.shape, f32),
            jax.ShapeDtypeStruct(cores.shape, f32),
        ),
        in_specs=[vm] * 3,
        out_specs=(vm,) * 4,
        scratch_shapes=[
            pltpu.VMEM((panels, order, B), f32),
            pltpu.VMEM((rmax, order), f32),
            pltpu.VMEM((order, order), f32),
            pltpu.VMEM((B, B), f32),
            pltpu.VMEM((B, B), f32),
            pltpu.VMEM((B, B), f32),
            pltpu.VMEM((rmax, rmax), f32),
            pltpu.VMEM((span, rmax, rmax), f32),
            pltpu.VMEM((rmax, order), f32),
            pltpu.VMEM((order, rmax), f32),
            dma((tiles // 2, panels)),
            dma((panels,)),
            dma((panels, 2, layers)),
            dma((panels, layers)),
            dma((tiles // 2,)),
            dma,
            dma((layers,)),
            dma,
            dma((tiles,)),
            dma((span,)),
        ],
        compiler_params=pltpu.CompilerParams(collective_id=0, has_side_effects=True),
    )(diag, masked_t, cores)
    return factors, zt.T[None], schur, couplings


def solution(mesh):
    placed = (
        P("tile", None, None),
        P("tile"),
        P("tile", "layer", None, None),
        P("tile", "layer", None),
    )
    return jax.shard_map(
        functools.partial(body, mesh.shape["tile"], mesh.shape["layer"]),
        mesh=mesh,
        in_specs=placed,
        out_specs=(
            P(None, "layer", None),
            P(),
            P("tile", "layer", None),
            P("tile", "layer", None, None),
        ),
        check_vma=False,
    )
```
